32 devices in a mesh: seq: 4 (over y, x), feat: 8 (over z, core).
Axes of the slice: x: 2, y: 2, z: 4, core: 2. Of those that a mesh axis runs over, the one named last changes fastest.
Arguments:
- queries: bfloat16 [3840, 16, 128], P('seq'), may hold values from -32 to 32
- key_vectors: bfloat16 [3840, 16, 128], P('seq'), may hold values from -32 to 32
- values: bfloat16 [3840, 16, 128], P('seq'), may hold values from -6 to 6
- projections: bfloat16 [16, 4096, 128], P(None, 'feat'), may hold values from -4 to 4
Outputs:
- attended: bfloat16 [3840, 16, 128], P('seq', 'feat')
The draws below stay inside these ranges and needn't reach their ends.
All inputs are finite; a program needn't handle non-finite values.
Results may differ from the reference program's by a relative error of at most 0.012.
Values may be sent and summed in bfloat16 or wider, within the bound.
A program may use at most 128 MiB of HBM per device.

```python
import jax
import jax.numpy as jnp
from jax import lax

H = 16
E = 128
M = 4096
TOKENS = 3840


def scaled_rows(key):
    base = jnp.clip(jax.random.normal(jax.random.fold_in(key, 11), (TOKENS, H, E), jnp.float32), -4.0, 4.0)
    return base.astype(jnp.bfloat16)


def draw_queries(key, part):
    return scaled_rows(jax.random.fold_in(key, 101))


def draw_key_vectors(key, part):
    return scaled_rows(jax.random.fold_in(key, 202))


def block_scale(own_key, dims, cuts, least, top_value):
    loudness = 1.0
    for dim, parts in cuts:
        steps = jax.random.uniform(jax.random.fold_in(jax.random.fold_in(own_key, 6), dim), (parts,), jnp.float32, least / len(cuts), top_value / len(cuts))
        loudness = loudness * jnp.repeat(jnp.exp(steps), dims[dim] // parts).reshape((-1,) + (1,) * (len(dims) - 1 - dim))
    return loudness


def normal_values(stream_key, dims, width, reach, split=(), held_as=jnp.bfloat16):
    gain = block_scale(stream_key, dims, split, -0.22, 0.18) if split else 1.0
    drawn = jax.random.normal(stream_key, dims, jnp.float32) * width * gain
    return jnp.minimum(jnp.maximum(drawn, -reach), reach).astype(held_as)


def setup_inputs(seed: int = 0) -> dict:
    seeds = jax.random.split(jax.random.key(seed), 5)
    queries = draw_queries(jax.random.fold_in(seeds[4], 71), 0)
    key_vectors = draw_key_vectors(jax.random.fold_in(seeds[4], 71), 0)
    values = normal_values(seeds[2], (TOKENS, H, E), 1.0, 6.0, ((0, 4),))
    projections = normal_values(seeds[3], (H, M, E), 1.0, 4.0, ((1, 8),))
    return dict(queries=queries, key_vectors=key_vectors, values=values, projections=projections)


def head_attend(pieces):
    query_rows, key_rows, value_rows, omega_rows = pieces
    scaling = E ** -0.25
    key_dash = jnp.dot(key_rows, omega_rows.T, preferred_element_type=jnp.float32) * scaling
    key_diag = jnp.sum(jnp.square(key_rows.astype(jnp.float32)), axis=1) * (0.5 * scaling * scaling)
    key_expo = key_dash - key_diag[:, None]
    key_phi = jnp.exp(key_expo - jnp.max(key_expo)).astype(jnp.bfloat16)
    key_state = jnp.dot(key_phi.T, value_rows, preferred_element_type=jnp.float32)
    key_mass = jnp.sum(key_phi.astype(jnp.float32), axis=0)
    query_dash = jnp.dot(query_rows, omega_rows.T, preferred_element_type=jnp.float32) * scaling
    query_phi = jnp.exp(query_dash - jnp.max(query_dash, axis=1, keepdims=True)).astype(jnp.bfloat16)
    numerator = jnp.dot(query_phi, key_state.astype(jnp.bfloat16), preferred_element_type=jnp.float32)
    denominator = jnp.dot(query_phi.astype(jnp.float32), key_mass, precision=lax.Precision.HIGHEST)
    return (numerator / denominator[:, None]).astype(jnp.bfloat16)


def reference(queries, key_vectors, values, projections):
    stacked = lax.map(head_attend, (jnp.swapaxes(queries, 0, 1), jnp.swapaxes(key_vectors, 0, 1), jnp.swapaxes(values, 0, 1), projections))
    return jnp.swapaxes(stacked, 0, 1)
```

```python
import functools
import math

import jax
import jax.numpy as jnp
from jax import lax
from jax.experimental import pallas as pl
from jax.experimental.pallas import tpu as pltpu
from jax.sharding import PartitionSpec as P

E = 128
AHEAD = 2
BEHIND = 1


def key_exponents(key_vectors, directions, scaling):
    key_dash = (
        jnp.einsum("the,hme->thm", key_vectors, directions, preferred_element_type=jnp.float32)
        * scaling
    )
    key_diag = jnp.sum(jnp.square(key_vectors.astype(jnp.float32)), axis=2) * (
        0.5 * scaling * scaling
    )
    return key_dash - key_diag[:, :, None]


def key_terms(key_expo, key_peak, values):
    key_phi = jnp.exp(key_expo - key_peak[None, :, None]).astype(jnp.bfloat16)
    key_state = jnp.einsum("thm,the->hme", key_phi, values, preferred_element_type=jnp.float32)
    key_mass = jnp.sum(key_phi, axis=0, dtype=jnp.float32)
    return (key_state, key_mass)


def partial_output(query_dash, query_peak, state_half, key_mass):
    query_phi = jnp.exp(query_dash - query_peak[:, :, None]).astype(jnp.bfloat16)
    numerator = jnp.einsum(
        "thm,hme->the", query_phi, state_half, preferred_element_type=jnp.float32
    )
    denominator = jnp.einsum(
        "thm,hm->th", query_phi.astype(jnp.float32), key_mass, precision=lax.Precision.HIGHEST
    )
    return (numerator, denominator)


def shards(queries, key_vectors, values, projections):
    scaling = E ** (-0.25)
    directions = lax.all_to_all(projections, "feat", split_axis=0, concat_axis=1, tiled=True)
    head_share = queries.shape[1] // lax.axis_size("feat")
    start_head = lax.axis_index("feat") * head_share
    own_queries = lax.dynamic_slice_in_dim(queries, start_head, head_share, 1)
    own_keys = lax.dynamic_slice_in_dim(key_vectors, start_head, head_share, 1)
    own_values = lax.dynamic_slice_in_dim(values, start_head, head_share, 1)
    key_expo = key_exponents(own_keys, directions, scaling)
    key_peak = lax.pmax(jnp.max(key_expo, axis=(0, 2)), "seq")
    key_state, key_mass = key_terms(key_expo, key_peak, own_values)
    key_state, key_mass = lax.psum((key_state, key_mass), "seq")
    state_half = key_state.astype(jnp.bfloat16)
    query_dash = (
        jnp.einsum("the,hme->thm", own_queries, directions, preferred_element_type=jnp.float32)
        * scaling
    )
    numerator, denominator = partial_output(
        query_dash, jnp.max(query_dash, axis=2), state_half, key_mass
    )
    return (numerator / denominator[:, :, None]).astype(jnp.bfloat16)


MESH = pl.DeviceIdType.MESH
LOW = -1e30


def dot_nt(a, b):
    return lax.dot_general(a, b, (((1,), (1,)), ((), ())), preferred_element_type=jnp.float32)


def flip(index, bits, width):
    out = index
    bit = 1
    while bit < width:
        if bits & bit:
            out = out + bit * (1 - 2 * ((index // bit) % 2))
        bit *= 2
    return out


def head_kernel(
    chunks, ahead, behind, scale,
    q_hbm, k_hbm, v_hbm, dirs_hbm, out_ref,
    q_ref, k_ref, v_ref, diag_ref, w_ref,
    state_ref, peak_ref, send_ref, recv_ref, send_aux, recv_aux,
    acc_ref, row_ref, top_ref, result_ref,
    load_sem, x_send, x_recv, w_send, w_recv, y_send, y_recv, o_send, o_recv,
):
    tokens, size = k_ref.shape[1:]
    width = w_ref.shape[1]
    groups = width // size
    seq = lax.axis_index("seq")
    feat = lax.axis_index("feat")
    side = seq % 2
    x_mate = flip(seq, 1, 4)
    y_mate = flip(seq, 2, 4)
    mates = [flip(feat, bits, chunks) for bits in range(1, chunks)]

    own_loads = [
        pltpu.make_async_copy(k_hbm.at[side], k_ref.at[0], load_sem.at[0]),
        pltpu.make_async_copy(v_hbm.at[side], v_ref.at[0], load_sem.at[1]),
        pltpu.make_async_copy(q_hbm.at[side], q_ref.at[0], load_sem.at[2]),
        pltpu.make_async_copy(dirs_hbm.at[feat * 2 + side], w_ref.at[0], w_recv.at[0]),
    ]
    for load in own_loads:
        load.start()

    barrier = pltpu.get_barrier_semaphore()
    pl.semaphore_signal(barrier, inc=1, device_id={"seq": x_mate}, device_id_type=MESH)
    pl.semaphore_signal(barrier, inc=1, device_id={"seq": y_mate}, device_id_type=MESH)
    for mate in mates:
        pl.semaphore_signal(barrier, inc=1, device_id={"feat": mate}, device_id_type=MESH)
    pl.semaphore_wait(barrier, 1 + chunks)

    x_copies = []
    for i, (src, dst) in enumerate(((k_hbm, k_ref), (v_hbm, v_ref), (q_hbm, q_ref))):
        x_copies.append(pltpu.make_async_remote_copy(
            src_ref=src.at[1 - side], dst_ref=dst.at[1],
            send_sem=x_send.at[i], recv_sem=x_recv.at[i],
            device_id={"seq": x_mate}, device_id_type=MESH))
    w_copies = []
    for i, mate in enumerate(mates):
        w_copies.append(pltpu.make_async_remote_copy(
            src_ref=dirs_hbm.at[mate * 2 + side], dst_ref=w_ref.at[i + 1],
            send_sem=w_send.at[i + 1], recv_sem=w_recv.at[i + 1],
            device_id={"feat": mate}, device_id_type=MESH))
    for copy in x_copies[:2] + w_copies + x_copies[2:]:
        copy.start()

    def state_copies(slot):
        return [
            pltpu.make_async_remote_copy(
                src_ref=send_ref.at[slot], dst_ref=recv_ref.at[slot],
                send_sem=y_send.at[0, slot], recv_sem=y_recv.at[0, slot],
                device_id={"seq": y_mate}, device_id_type=MESH),
            pltpu.make_async_remote_copy(
                src_ref=send_aux.at[slot], dst_ref=recv_aux.at[slot],
                send_sem=y_send.at[1, slot], recv_sem=y_recv.at[1, slot],
                device_id={"seq": y_mate}, device_id_type=MESH),
        ]

    acc_ref[...] = jnp.zeros_like(acc_ref)
    row_ref[...] = jnp.full_like(row_ref, LOW)
    top_ref[...] = jnp.full_like(top_ref, LOW)

    lane_t = lax.broadcasted_iota(jnp.int32, (tokens, size), 1)
    lane_w = lax.broadcasted_iota(jnp.int32, (width, size), 1)
    minus = jnp.where(lane_w < 3, -1.0, 0.0).astype(jnp.bfloat16)
    ones = jnp.ones((16, tokens), jnp.bfloat16)

    def make_diag(half):
        key = k_ref[half].astype(jnp.float32)
        full = jnp.sum(key * key, axis=1, keepdims=True) * (0.5 * scale)
        high = full.astype(jnp.bfloat16).astype(jnp.float32)
        rest = full - high
        mid = rest.astype(jnp.bfloat16).astype(jnp.float32)
        low = rest - mid
        block = jnp.where(lane_t == 0, high, jnp.where(lane_t == 1, mid, jnp.where(lane_t == 2, low, 0.0)))
        diag_ref[half] = block.astype(jnp.bfloat16)

    slope = scale * math.log2(math.e)

    def key_unit(half, slot):
        keys = jnp.concatenate([k_ref[half], diag_ref[half]], axis=1)
        dirs = jnp.concatenate([w_ref[slot], minus], axis=1)
        raw = dot_nt(keys, dirs)
        peak = jnp.max(raw, axis=0, keepdims=True)
        if half == 1:
            before = peak_ref[slot, 0:1, :]
            peak = jnp.maximum(peak, before)
        phi = jnp.exp2((raw - peak) * slope).astype(jnp.bfloat16)
        vals = jnp.concatenate([v_ref[half], ones], axis=0)
        state = jnp.dot(vals, phi, preferred_element_type=jnp.float32)
        if half == 1:
            state = state + state_ref[slot] * jnp.exp2((before - peak) * slope)
        state_ref[slot] = state
        peak_ref[slot, 0:1, :] = peak
        if half == 1:
            send_ref[slot] = state[:size].astype(jnp.bfloat16)
            for g in range(groups):
                cut = slice(g * size, (g + 1) * size)
                send_aux[slot, g:g + 1, :] = state[size:size + 1, cut]
                send_aux[slot, groups + g:groups + g + 1, :] = peak[:, cut]

    def query_unit(slot):
        own_peak = peak_ref[slot, 0:1, :]
        got_peak = jnp.concatenate([recv_aux[slot, groups + g:groups + g + 1, :] for g in range(groups)], axis=1)
        got_mass = jnp.concatenate([recv_aux[slot, g:g + 1, :] for g in range(groups)], axis=1)
        before = top_ref[0:1, 0:1]
        top = jnp.maximum(before, jnp.max(jnp.maximum(own_peak, got_peak), axis=1, keepdims=True))
        top_ref[...] = jnp.broadcast_to(top, top_ref.shape)
        own_gain = jnp.exp2((own_peak - top) * slope)
        got_gain = jnp.exp2((got_peak - top) * slope)
        state = (state_ref[slot, 0:size, :] * own_gain + recv_ref[slot].astype(jnp.float32) * got_gain).astype(jnp.bfloat16)
        mass = state_ref[slot, size:size + 1, :] * own_gain + got_mass * got_gain
        high = mass.astype(jnp.bfloat16).astype(jnp.float32)
        table = jnp.concatenate([
            state,
            jnp.broadcast_to(high, (size // 2, width)).astype(jnp.bfloat16),
            jnp.broadcast_to(mass - high, (size // 2, width)).astype(jnp.bfloat16)], axis=0)
        drop = (before - top) * slope

        def one_half(half, carry):
            raw = dot_nt(q_ref[half], w_ref[slot])
            last = row_ref[half]
            peak = jnp.maximum(last, jnp.max(raw, axis=1, keepdims=True))
            row_ref[half] = peak
            wide = jnp.concatenate([peak] * groups, axis=1)
            phi = jnp.exp2((raw - wide) * slope).astype(jnp.bfloat16)
            part = dot_nt(phi, table)
            fade = jnp.exp2((last - peak) * slope + drop)
            acc_ref[half] = acc_ref[half] * jnp.concatenate([fade, fade], axis=1) + part
            return carry

        lax.fori_loop(0, 2, one_half, 0)

    def finish(half):
        numer = acc_ref[half, :, 0:size]
        denom = acc_ref[half, :, size:2 * size]
        denom = denom + pltpu.roll(denom, size // 2, 1)
        return (numer / denom).astype(jnp.bfloat16)

    def step(t, carry):
        @pl.when(t < chunks)
        def _():
            pltpu.make_async_copy(w_ref.at[t], w_ref.at[t], w_recv.at[t]).wait()
            key_unit(0, t)

        @pl.when(t == ahead)
        def _():
            x_copies[0].wait_recv()
            x_copies[1].wait_recv()
            make_diag(1)

        @pl.when((t >= ahead) & (t < ahead + chunks))
        def _():
            key_unit(1, t - ahead)
            for copy in state_copies(t - ahead):
                copy.start()

        @pl.when(t == ahead + behind)
        def _():
            own_loads[2].wait()
            x_copies[2].wait_recv()

        @pl.when(t >= ahead + behind)
        def _():
            slot = t - ahead - behind
            for copy in state_copies(slot):
                copy.wait_recv()
            query_unit(slot)

        return carry

    own_loads[0].wait()
    own_loads[1].wait()
    make_diag(0)
    lax.fori_loop(0, chunks + ahead + behind, step, 0)

    result_ref[...] = finish(1)
    out_copy = pltpu.make_async_remote_copy(
        src_ref=result_ref, dst_ref=out_ref.at[side], send_sem=o_send, recv_sem=o_recv,
        device_id={"seq": x_mate}, device_id_type=MESH)
    out_copy.start()
    out_ref[side] = finish(0)
    for copy in x_copies:
        copy.wait_send()
    for copy in w_copies:
        copy.wait_send()

    def drain(t, carry):
        for copy in state_copies(t):
            copy.wait_send()
        return carry

    lax.fori_loop(0, chunks, drain, 0)
    out_copy.wait()


def paired_shards(chunks, queries, key_vectors, values, projections):
    tokens, _, size = queries.shape
    width = projections.shape[1]
    scale = size ** -0.25
    start = lax.axis_index("feat") * 2
    pair = [lax.dynamic_slice_in_dim(a, start, 2, 1) for a in (queries, key_vectors, values)]
    own_q, own_k = (jnp.transpose(a, (1, 0, 2)) for a in pair[:2])
    own_v = jnp.transpose(pair[2], (1, 2, 0))
    bf16, f32 = jnp.bfloat16, jnp.float32
    dma = pltpu.SemaphoreType.DMA
    out = pl.pallas_call(
        functools.partial(head_kernel, chunks, AHEAD, BEHIND, scale),
        out_shape=jax.ShapeDtypeStruct((2, tokens, size), bf16),
        in_specs=[pl.BlockSpec(memory_space=pl.ANY)] * 4,
        out_specs=pl.BlockSpec(memory_space=pltpu.VMEM),
        scratch_shapes=[
            pltpu.VMEM((2, tokens, size), bf16),
            pltpu.VMEM((2, tokens, size), bf16),
            pltpu.VMEM((2, size, tokens), bf16),
            pltpu.VMEM((2, tokens, size), bf16),
            pltpu.VMEM((chunks, width, size), bf16),
            pltpu.VMEM((chunks, size + 16, width), f32),
            pltpu.VMEM((chunks, 8, width), f32),
            pltpu.VMEM((chunks, size, width), bf16),
            pltpu.VMEM((chunks, size, width), bf16),
            pltpu.VMEM((chunks, 2 * (width // size), size), f32),
            pltpu.VMEM((chunks, 2 * (width // size), size), f32),
            pltpu.VMEM((2, tokens, 2 * size), f32),
            pltpu.VMEM((2, tokens, size), f32),
            pltpu.VMEM((8, size), f32),
            pltpu.VMEM((tokens, size), bf16),
            dma((3,)), dma((3,)), dma((3,)), dma((chunks,)), dma((chunks,)),
            dma((2, chunks)), dma((2, chunks)), dma, dma,
        ],
        compiler_params=pltpu.CompilerParams(
            collective_id=0, has_side_effects=True, vmem_limit_bytes=60 * 1024 * 1024),
        name="favor_heads",
    )(own_q, own_k, own_v, projections)
    return jnp.transpose(out, (1, 0, 2))


def pairs_fit(mesh, args):
    queries, _, _, projections = args
    seq, feat = mesh.shape["seq"], mesh.shape["feat"]
    width = projections.shape[1] // feat
    tokens, size = queries.shape[0] // seq, queries.shape[2]
    return (seq == 4 and feat & (feat - 1) == 0 and queries.shape[1] == 2 * feat
            and size == 128 and width % size == 0 and tokens % 16 == 0)


def solution(mesh):
    placed = (
        P("seq", None, None),
        P("seq", None, None),
        P("seq", None, None),
        P(None, "feat", None),
    )

    def run(*args):
        body = functools.partial(paired_shards, mesh.shape["feat"]) if pairs_fit(mesh, args) else shards
        return jax.shard_map(
            body, mesh=mesh, in_specs=placed, out_specs=P("seq", "feat", None), check_vma=False
        )(*args)

    return run
```

```python
import functools
import math

import jax
import jax.numpy as jnp
from jax import lax
from jax.experimental import pallas as pl
from jax.experimental.pallas import tpu as pltpu
from jax.sharding import PartitionSpec as P

E = 128
AHEAD = 1
BEHIND = 3
LATE = 2


def key_exponents(key_vectors, directions, scaling):
    key_dash = (
        jnp.einsum("the,hme->thm", key_vectors, directions, preferred_element_type=jnp.float32)
        * scaling
    )
    key_diag = jnp.sum(jnp.square(key_vectors.astype(jnp.float32)), axis=2) * (
        0.5 * scaling * scaling
    )
    return key_dash - key_diag[:, :, None]


def key_terms(key_expo, key_peak, values):
    key_phi = jnp.exp(key_expo - key_peak[None, :, None]).astype(jnp.bfloat16)
    key_state = jnp.einsum("thm,the->hme", key_phi, values, preferred_element_type=jnp.float32)
    key_mass = jnp.sum(key_phi, axis=0, dtype=jnp.float32)
    return (key_state, key_mass)


def partial_output(query_dash, query_peak, state_half, key_mass):
    query_phi = jnp.exp(query_dash - query_peak[:, :, None]).astype(jnp.bfloat16)
    numerator = jnp.einsum(
        "thm,hme->the", query_phi, state_half, preferred_element_type=jnp.float32
    )
    denominator = jnp.einsum(
        "thm,hm->th", query_phi.astype(jnp.float32), key_mass, precision=lax.Precision.HIGHEST
    )
    return (numerator, denominator)


def shards(queries, key_vectors, values, projections):
    scaling = E ** (-0.25)
    directions = lax.all_to_all(projections, "feat", split_axis=0, concat_axis=1, tiled=True)
    head_share = queries.shape[1] // lax.axis_size("feat")
    start_head = lax.axis_index("feat") * head_share
    own_queries = lax.dynamic_slice_in_dim(queries, start_head, head_share, 1)
    own_keys = lax.dynamic_slice_in_dim(key_vectors, start_head, head_share, 1)
    own_values = lax.dynamic_slice_in_dim(values, start_head, head_share, 1)
    key_expo = key_exponents(own_keys, directions, scaling)
    key_peak = lax.pmax(jnp.max(key_expo, axis=(0, 2)), "seq")
    key_state, key_mass = key_terms(key_expo, key_peak, own_values)
    key_state, key_mass = lax.psum((key_state, key_mass), "seq")
    state_half = key_state.astype(jnp.bfloat16)
    query_dash = (
        jnp.einsum("the,hme->thm", own_queries, directions, preferred_element_type=jnp.float32)
        * scaling
    )
    numerator, denominator = partial_output(
        query_dash, jnp.max(query_dash, axis=2), state_half, key_mass
    )
    return (numerator / denominator[:, :, None]).astype(jnp.bfloat16)


MESH = pl.DeviceIdType.MESH
LOW = -1e30


def dot_nt(a, b):
    return lax.dot_general(a, b, (((1,), (1,)), ((), ())), preferred_element_type=jnp.float32)


def flip(index, bits, width):
    out = index
    bit = 1
    while bit < width:
        if bits & bit:
            out = out + bit * (1 - 2 * ((index // bit) % 2))
        bit *= 2
    return out


def head_kernel(
    chunks, ahead, behind, late, scale,
    q_hbm, k_hbm, v_hbm, dirs_hbm, out_ref,
    q_ref, k_ref, v_ref, diag_ref, w_ref,
    state_ref, peak_ref, send_ref, recv_ref, send_aux, recv_aux,
    acc_ref, row_ref, top_ref, drop_ref, table_ref, result_ref,
    load_sem, x_send, x_recv, w_send, w_recv, y_send, y_recv, o_send, o_recv,
):
    tokens, size = k_ref.shape[1:]
    width = w_ref.shape[1]
    groups = width // size
    seq = lax.axis_index("seq")
    feat = lax.axis_index("feat")
    low, high = seq % 2, seq // 2
    odd = feat % 2
    side = low * (1 - odd) + high * odd
    low_step, high_step = 1 - 2 * low, 2 - 4 * high
    x_mate = seq + low_step * (1 - odd) + high_step * odd
    y_mate = seq + low_step * odd + high_step * (1 - odd)
    mates = [flip(feat, bits, chunks) for bits in range(1, chunks)]

    own_loads = [
        pltpu.make_async_copy(k_hbm.at[side], k_ref.at[0], load_sem.at[0]),
        pltpu.make_async_copy(v_hbm.at[side], v_ref.at[0], load_sem.at[1]),
        pltpu.make_async_copy(q_hbm.at[side], q_ref.at[0], load_sem.at[2]),
        pltpu.make_async_copy(dirs_hbm.at[feat * 2 + side], w_ref.at[0], w_recv.at[0]),
    ]
    for load in own_loads:
        load.start()

    barrier = pltpu.get_barrier_semaphore()
    pl.semaphore_signal(barrier, inc=1, device_id={"seq": x_mate}, device_id_type=MESH)
    pl.semaphore_signal(barrier, inc=1, device_id={"seq": y_mate}, device_id_type=MESH)
    for mate in mates:
        pl.semaphore_signal(barrier, inc=1, device_id={"feat": mate}, device_id_type=MESH)
    pl.semaphore_wait(barrier, 1 + chunks)

    x_copies = []
    for i, (src, dst) in enumerate(((k_hbm, k_ref), (v_hbm, v_ref), (q_hbm, q_ref))):
        x_copies.append(pltpu.make_async_remote_copy(
            src_ref=src.at[1 - side], dst_ref=dst.at[1],
            send_sem=x_send.at[i], recv_sem=x_recv.at[i],
            device_id={"seq": x_mate}, device_id_type=MESH))
    w_copies = []
    for i, mate in enumerate(mates):
        w_copies.append(pltpu.make_async_remote_copy(
            src_ref=dirs_hbm.at[mate * 2 + low * (1 - mate % 2) + high * (mate % 2)], dst_ref=w_ref.at[i + 1],
            send_sem=w_send.at[i + 1], recv_sem=w_recv.at[i + 1],
            device_id={"feat": mate}, device_id_type=MESH))
    for copy in x_copies[:2] + w_copies + x_copies[2:]:
        copy.start()

    def state_copies(slot):
        return [
            pltpu.make_async_remote_copy(
                src_ref=send_ref.at[slot], dst_ref=recv_ref.at[slot],
                send_sem=y_send.at[0, slot], recv_sem=y_recv.at[0, slot],
                device_id={"seq": y_mate}, device_id_type=MESH),
            pltpu.make_async_remote_copy(
                src_ref=send_aux.at[slot], dst_ref=recv_aux.at[slot],
                send_sem=y_send.at[1, slot], recv_sem=y_recv.at[1, slot],
                device_id={"seq": y_mate}, device_id_type=MESH),
        ]

    acc_ref[...] = jnp.zeros_like(acc_ref)
    row_ref[...] = jnp.full_like(row_ref, LOW)
    top_ref[...] = jnp.full_like(top_ref, LOW)

    lane_t = lax.broadcasted_iota(jnp.int32, (tokens, size), 1)
    lane_w = lax.broadcasted_iota(jnp.int32, (width, size), 1)
    minus = jnp.where(lane_w < 3, -1.0, 0.0).astype(jnp.bfloat16)
    ones = jnp.ones((16, tokens), jnp.bfloat16)

    def make_diag(half):
        key = k_ref[half].astype(jnp.float32)
        full = jnp.sum(key * key, axis=1, keepdims=True) * (0.5 * scale)
        high = full.astype(jnp.bfloat16).astype(jnp.float32)
        rest = full - high
        mid = rest.astype(jnp.bfloat16).astype(jnp.float32)
        low = rest - mid
        block = jnp.where(lane_t == 0, high, jnp.where(lane_t == 1, mid, jnp.where(lane_t == 2, low, 0.0)))
        diag_ref[half] = block.astype(jnp.bfloat16)

    slope = scale * math.log2(math.e)

    def key_unit(half, slot):
        keys = jnp.concatenate([k_ref[half], diag_ref[half]], axis=1)
        dirs = jnp.concatenate([w_ref[slot], minus], axis=1)
        raw = dot_nt(keys, dirs)
        peak = jnp.max(raw, axis=0, keepdims=True)
        if half == 1:
            before = peak_ref[slot, 0:1, :]
            peak = jnp.maximum(peak, before)
        phi = jnp.exp2((raw - peak) * slope).astype(jnp.bfloat16)
        vals = jnp.concatenate([v_ref[half], ones], axis=0)
        state = jnp.dot(vals, phi, preferred_element_type=jnp.float32)
        if half == 1:
            state = state + state_ref[slot] * jnp.exp2((before - peak) * slope)
        state_ref[slot] = state
        peak_ref[slot, 0:1, :] = peak
        if half == 1:
            send_ref[slot] = state[:size].astype(jnp.bfloat16)
            for g in range(groups):
                cut = slice(g * size, (g + 1) * size)
                send_aux[slot, g:g + 1, :] = state[size:size + 1, cut]
                send_aux[slot, groups + g:groups + g + 1, :] = peak[:, cut]

    def combine(slot):
        own_peak = peak_ref[slot, 0:1, :]
        got_peak = jnp.concatenate([recv_aux[slot, groups + g:groups + g + 1, :] for g in range(groups)], axis=1)
        got_mass = jnp.concatenate([recv_aux[slot, g:g + 1, :] for g in range(groups)], axis=1)
        before = top_ref[0:1, 0:1]
        top = jnp.maximum(before, jnp.max(jnp.maximum(own_peak, got_peak), axis=1, keepdims=True))
        top_ref[...] = jnp.broadcast_to(top, top_ref.shape)
        drop_ref[slot] = jnp.broadcast_to((before - top) * slope, drop_ref.shape[1:])
        own_gain = jnp.exp2((own_peak - top) * slope)
        got_gain = jnp.exp2((got_peak - top) * slope)
        state = state_ref[slot, 0:size, :] * own_gain + recv_ref[slot].astype(jnp.float32) * got_gain
        mass = state_ref[slot, size:size + 1, :] * own_gain + got_mass * got_gain
        coarse = mass.astype(jnp.bfloat16).astype(jnp.float32)
        table_ref[slot, 0:size, :] = state.astype(jnp.bfloat16)
        half_shape = (size // 2, width)
        table_ref[slot, size:size + size // 2, :] = jnp.broadcast_to(coarse, half_shape).astype(jnp.bfloat16)
        table_ref[slot, size + size // 2:2 * size, :] = jnp.broadcast_to(mass - coarse, half_shape).astype(jnp.bfloat16)

    def query_unit(half, slot):
        raw = dot_nt(q_ref[half], w_ref[slot])
        last = row_ref[half]
        peak = jnp.maximum(last, jnp.max(raw, axis=1, keepdims=True))
        row_ref[half] = peak
        wide = jnp.concatenate([peak] * groups, axis=1)
        phi = jnp.exp2((raw - wide) * slope).astype(jnp.bfloat16)
        part = dot_nt(phi, table_ref[slot])
        fade = jnp.exp2((last - peak) * slope + drop_ref[slot, 0:1, :])
        acc_ref[half] = acc_ref[half] * jnp.concatenate([fade, fade], axis=1) + part

    def finish(half):
        numer = acc_ref[half, :, 0:size]
        denom = acc_ref[half, :, size:2 * size]
        denom = denom + pltpu.roll(denom, size // 2, 1)
        return (numer / denom).astype(jnp.bfloat16)

    def step(t, carry):
        @pl.when(t < chunks)
        def _():
            pltpu.make_async_copy(w_ref.at[t], w_ref.at[t], w_recv.at[t]).wait()
            key_unit(0, t)

        @pl.when(t == ahead)
        def _():
            x_copies[0].wait_recv()
            x_copies[1].wait_recv()
            make_diag(1)

        @pl.when((t >= ahead) & (t < ahead + chunks))
        def _():
            key_unit(1, t - ahead)
            for copy in state_copies(t - ahead):
                copy.start()

        @pl.when(t == ahead + behind)
        def _():
            own_loads[2].wait()
            x_copies[2].wait_recv()

        @pl.when((t >= ahead + behind) & (t < ahead + behind + chunks))
        def _():
            slot = t - ahead - behind
            for copy in state_copies(slot):
                copy.wait_recv()
            combine(slot)
            query_unit(1, slot)

        @pl.when(t == ahead + behind + chunks - 1)
        def _():
            result_ref[...] = finish(1)
            out_copy.start()

        @pl.when(t >= ahead + behind + late)
        def _():
            query_unit(0, t - ahead - behind - late)

        return carry

    out_copy = pltpu.make_async_remote_copy(
        src_ref=result_ref, dst_ref=out_ref.at[side], send_sem=o_send, recv_sem=o_recv,
        device_id={"seq": x_mate}, device_id_type=MESH)
    own_loads[0].wait()
    own_loads[1].wait()
    make_diag(0)
    lax.fori_loop(0, chunks + ahead + behind + late, step, 0)
    out_ref[side] = finish(0)
    for copy in x_copies:
        copy.wait_send()
    for copy in w_copies:
        copy.wait_send()

    def drain(t, carry):
        for copy in state_copies(t):
            copy.wait_send()
        return carry

    lax.fori_loop(0, chunks, drain, 0)
    out_copy.wait()


def paired_shards(chunks, queries, key_vectors, values, projections):
    tokens, _, size = queries.shape
    width = projections.shape[1]
    scale = size ** -0.25
    start = lax.axis_index("feat") * 2
    pair = [lax.dynamic_slice_in_dim(a, start, 2, 1) for a in (queries, key_vectors, values)]
    own_q, own_k = (jnp.transpose(a, (1, 0, 2)) for a in pair[:2])
    own_v = jnp.transpose(pair[2], (1, 2, 0))
    bf16, f32 = jnp.bfloat16, jnp.float32
    dma = pltpu.SemaphoreType.DMA
    out = pl.pallas_call(
        functools.partial(head_kernel, chunks, AHEAD, BEHIND, LATE, scale),
        out_shape=jax.ShapeDtypeStruct((2, tokens, size), bf16),
        in_specs=[pl.BlockSpec(memory_space=pl.ANY)] * 4,
        out_specs=pl.BlockSpec(memory_space=pltpu.VMEM),
        scratch_shapes=[
            pltpu.VMEM((2, tokens, size), bf16),
            pltpu.VMEM((2, tokens, size), bf16),
            pltpu.VMEM((2, size, tokens), bf16),
            pltpu.VMEM((2, tokens, size), bf16),
            pltpu.VMEM((chunks, width, size), bf16),
            pltpu.VMEM((chunks, size + 16, width), f32),
            pltpu.VMEM((chunks, 8, width), f32),
            pltpu.VMEM((chunks, size, width), bf16),
            pltpu.VMEM((chunks, size, width), bf16),
            pltpu.VMEM((chunks, 2 * (width // size), size), f32),
            pltpu.VMEM((chunks, 2 * (width // size), size), f32),
            pltpu.VMEM((2, tokens, 2 * size), f32),
            pltpu.VMEM((2, tokens, size), f32),
            pltpu.VMEM((8, size), f32),
            pltpu.VMEM((chunks, 8, size), f32),
            pltpu.VMEM((chunks, 2 * size, width), bf16),
            pltpu.VMEM((tokens, size), bf16),
            dma((3,)), dma((3,)), dma((3,)), dma((chunks,)), dma((chunks,)),
            dma((2, chunks)), dma((2, chunks)), dma, dma,
        ],
        compiler_params=pltpu.CompilerParams(
            collective_id=0, has_side_effects=True, vmem_limit_bytes=60 * 1024 * 1024),
        name="favor_heads",
    )(own_q, own_k, own_v, projections)
    return jnp.transpose(out, (1, 0, 2))


def pairs_fit(mesh, args):
    queries, _, _, projections = args
    seq, feat = mesh.shape["seq"], mesh.shape["feat"]
    width = projections.shape[1] // feat
    tokens, size = queries.shape[0] // seq, queries.shape[2]
    return (seq == 4 and feat & (feat - 1) == 0 and queries.shape[1] == 2 * feat
            and size == 128 and width % size == 0 and tokens % 16 == 0)


def solution(mesh):
    placed = (
        P("seq", None, None),
        P("seq", None, None),
        P("seq", None, None),
        P(None, "feat", None),
    )

    def run(*args):
        body = functools.partial(paired_shards, mesh.shape["feat"]) if pairs_fit(mesh, args) else shards
        return jax.shard_map(
            body, mesh=mesh, in_specs=placed, out_specs=P("seq", "feat", None), check_vma=False
        )(*args)

    return run
```

```python
import functools
import math

import jax
import jax.numpy as jnp
from jax import lax
from jax.experimental import pallas as pl
from jax.experimental.pallas import tpu as pltpu
from jax.sharding import PartitionSpec as P

E = 128
AHEAD = 1
BEHIND = 3
LATE = 3


def key_exponents(key_vectors, directions, scaling):
    key_dash = (
        jnp.einsum("the,hme->thm", key_vectors, directions, preferred_element_type=jnp.float32)
        * scaling
    )
    key_diag = jnp.sum(jnp.square(key_vectors.astype(jnp.float32)), axis=2) * (
        0.5 * scaling * scaling
    )
    return key_dash - key_diag[:, :, None]


def key_terms(key_expo, key_peak, values):
    key_phi = jnp.exp(key_expo - key_peak[None, :, None]).astype(jnp.bfloat16)
    key_state = jnp.einsum("thm,the->hme", key_phi, values, preferred_element_type=jnp.float32)
    key_mass = jnp.sum(key_phi, axis=0, dtype=jnp.float32)
    return (key_state, key_mass)


def partial_output(query_dash, query_peak, state_half, key_mass):
    query_phi = jnp.exp(query_dash - query_peak[:, :, None]).astype(jnp.bfloat16)
    numerator = jnp.einsum(
        "thm,hme->the", query_phi, state_half, preferred_element_type=jnp.float32
    )
    denominator = jnp.einsum(
        "thm,hm->th", query_phi.astype(jnp.float32), key_mass, precision=lax.Precision.HIGHEST
    )
    return (numerator, denominator)


def shards(queries, key_vectors, values, projections):
    scaling = E ** (-0.25)
    directions = lax.all_to_all(projections, "feat", split_axis=0, concat_axis=1, tiled=True)
    head_share = queries.shape[1] // lax.axis_size("feat")
    start_head = lax.axis_index("feat") * head_share
    own_queries = lax.dynamic_slice_in_dim(queries, start_head, head_share, 1)
    own_keys = lax.dynamic_slice_in_dim(key_vectors, start_head, head_share, 1)
    own_values = lax.dynamic_slice_in_dim(values, start_head, head_share, 1)
    key_expo = key_exponents(own_keys, directions, scaling)
    key_peak = lax.pmax(jnp.max(key_expo, axis=(0, 2)), "seq")
    key_state, key_mass = key_terms(key_expo, key_peak, own_values)
    key_state, key_mass = lax.psum((key_state, key_mass), "seq")
    state_half = key_state.astype(jnp.bfloat16)
    query_dash = (
        jnp.einsum("the,hme->thm", own_queries, directions, preferred_element_type=jnp.float32)
        * scaling
    )
    numerator, denominator = partial_output(
        query_dash, jnp.max(query_dash, axis=2), state_half, key_mass
    )
    return (numerator / denominator[:, :, None]).astype(jnp.bfloat16)


MESH = pl.DeviceIdType.MESH
LOW = -1e30


def dot_nt(a, b):
    return lax.dot_general(a, b, (((1,), (1,)), ((), ())), preferred_element_type=jnp.float32)


def flip(index, bits, width):
    out = index
    bit = 1
    while bit < width:
        if bits & bit:
            out = out + bit * (1 - 2 * ((index // bit) % 2))
        bit *= 2
    return out


def head_kernel(
    chunks, ahead, behind, late, scale,
    q_hbm, k_hbm, v_hbm, dirs_hbm, out_ref,
    q_ref, k_ref, v_ref, diag_ref, w_ref,
    state_ref, peak_ref, send_ref, recv_ref, send_aux, recv_aux,
    acc_ref, row_ref, top_ref, drop_ref, table_ref, result_ref,
    load_sem, x_send, x_recv, w_send, w_recv, y_send, y_recv, o_send, o_recv,
):
    tokens, size = k_ref.shape[1:]
    width = w_ref.shape[1]
    groups = width // size
    seq = lax.axis_index("seq")
    feat = lax.axis_index("feat")
    low, high = seq % 2, seq // 2
    odd = feat % 2
    side = low * (1 - odd) + high * odd
    low_step, high_step = 1 - 2 * low, 2 - 4 * high
    x_mate = seq + low_step * (1 - odd) + high_step * odd
    y_mate = seq + low_step * odd + high_step * (1 - odd)
    mates = [flip(feat, bits, chunks) for bits in range(1, chunks)]

    own_loads = [
        pltpu.make_async_copy(k_hbm.at[side], k_ref.at[0], load_sem.at[0]),
        pltpu.make_async_copy(v_hbm.at[side], v_ref.at[0], load_sem.at[1]),
        pltpu.make_async_copy(q_hbm.at[side], q_ref.at[0], load_sem.at[2]),
        pltpu.make_async_copy(dirs_hbm.at[feat * 2 + side], w_ref.at[0], w_recv.at[0]),
    ]
    for load in own_loads:
        load.start()

    barrier = pltpu.get_barrier_semaphore()
    pl.semaphore_signal(barrier, inc=1, device_id={"seq": x_mate}, device_id_type=MESH)
    pl.semaphore_signal(barrier, inc=1, device_id={"seq": y_mate}, device_id_type=MESH)
    for mate in mates:
        pl.semaphore_signal(barrier, inc=1, device_id={"feat": mate}, device_id_type=MESH)
    pl.semaphore_wait(barrier, 1 + chunks)

    x_copies = []
    for i, (src, dst) in enumerate(((k_hbm, k_ref), (v_hbm, v_ref), (q_hbm, q_ref))):
        x_copies.append(pltpu.make_async_remote_copy(
            src_ref=src.at[1 - side], dst_ref=dst.at[1],
            send_sem=x_send.at[i], recv_sem=x_recv.at[i],
            device_id={"seq": x_mate}, device_id_type=MESH))
    w_copies = []
    for i, mate in enumerate(mates):
        w_copies.append(pltpu.make_async_remote_copy(
            src_ref=dirs_hbm.at[mate * 2 + low * (1 - mate % 2) + high * (mate % 2)], dst_ref=w_ref.at[i + 1],
            send_sem=w_send.at[i + 1], recv_sem=w_recv.at[i + 1],
            device_id={"feat": mate}, device_id_type=MESH))
    for copy in x_copies[:2] + w_copies + x_copies[2:]:
        copy.start()

    def state_copies(slot):
        return [
            pltpu.make_async_remote_copy(
                src_ref=send_ref.at[slot], dst_ref=recv_ref.at[slot],
                send_sem=y_send.at[0, slot], recv_sem=y_recv.at[0, slot],
                device_id={"seq": y_mate}, device_id_type=MESH),
            pltpu.make_async_remote_copy(
                src_ref=send_aux.at[slot], dst_ref=recv_aux.at[slot],
                send_sem=y_send.at[1, slot], recv_sem=y_recv.at[1, slot],
                device_id={"seq": y_mate}, device_id_type=MESH),
        ]

    acc_ref[...] = jnp.zeros_like(acc_ref)
    row_ref[...] = jnp.full_like(row_ref, LOW)
    top_ref[...] = jnp.full_like(top_ref, LOW)

    lane_t = lax.broadcasted_iota(jnp.int32, (tokens, size), 1)
    lane_w = lax.broadcasted_iota(jnp.int32, (width, size), 1)
    minus = jnp.where(lane_w < 3, -1.0, 0.0).astype(jnp.bfloat16)
    ones = jnp.ones((16, tokens), jnp.bfloat16)

    def make_diag(half):
        key = k_ref[half].astype(jnp.float32)
        full = jnp.sum(key * key, axis=1, keepdims=True) * (0.5 * scale)
        high = full.astype(jnp.bfloat16).astype(jnp.float32)
        rest = full - high
        mid = rest.astype(jnp.bfloat16).astype(jnp.float32)
        low = rest - mid
        block = jnp.where(lane_t == 0, high, jnp.where(lane_t == 1, mid, jnp.where(lane_t == 2, low, 0.0)))
        diag_ref[half] = block.astype(jnp.bfloat16)

    slope = scale * math.log2(math.e)

    def key_unit(half, slot):
        keys = jnp.concatenate([k_ref[half], diag_ref[half]], axis=1)
        dirs = jnp.concatenate([w_ref[slot], minus], axis=1)
        raw = dot_nt(keys, dirs)
        peak = jnp.max(raw, axis=0, keepdims=True)
        if half == 1:
            before = peak_ref[slot, 0:1, :]
            peak = jnp.maximum(peak, before)
        phi = jnp.exp2((raw - peak) * slope).astype(jnp.bfloat16)
        vals = jnp.concatenate([v_ref[half], ones], axis=0)
        state = jnp.dot(vals, phi, preferred_element_type=jnp.float32)
        if half == 1:
            state = state + state_ref[slot] * jnp.exp2((before - peak) * slope)
        state_ref[slot] = state
        peak_ref[slot, 0:1, :] = peak
        if half == 1:
            send_ref[slot] = state[:size].astype(jnp.bfloat16)
            for g in range(groups):
                cut = slice(g * size, (g + 1) * size)
                send_aux[slot, g:g + 1, :] = state[size:size + 1, cut]
                send_aux[slot, groups + g:groups + g + 1, :] = peak[:, cut]

    def combine(slot):
        own_peak = peak_ref[slot, 0:1, :]
        got_peak = jnp.concatenate([recv_aux[slot, groups + g:groups + g + 1, :] for g in range(groups)], axis=1)
        got_mass = jnp.concatenate([recv_aux[slot, g:g + 1, :] for g in range(groups)], axis=1)
        before = top_ref[0:1, 0:1]
        top = jnp.maximum(before, jnp.max(jnp.maximum(own_peak, got_peak), axis=1, keepdims=True))
        top_ref[...] = jnp.broadcast_to(top, top_ref.shape)
        drop_ref[slot] = jnp.broadcast_to((before - top) * slope, drop_ref.shape[1:])
        own_gain = jnp.exp2((own_peak - top) * slope)
        got_gain = jnp.exp2((got_peak - top) * slope)
        state = state_ref[slot, 0:size, :] * own_gain + recv_ref[slot].astype(jnp.float32) * got_gain
        mass = state_ref[slot, size:size + 1, :] * own_gain + got_mass * got_gain
        coarse = mass.astype(jnp.bfloat16).astype(jnp.float32)
        table_ref[slot, 0:size, :] = state.astype(jnp.bfloat16)
        half_shape = (size // 2, width)
        table_ref[slot, size:size + size // 2, :] = jnp.broadcast_to(coarse, half_shape).astype(jnp.bfloat16)
        table_ref[slot, size + size // 2:2 * size, :] = jnp.broadcast_to(mass - coarse, half_shape).astype(jnp.bfloat16)

    def query_unit(half, slot):
        raw = dot_nt(q_ref[half], w_ref[slot])
        last = row_ref[half]
        peak = jnp.maximum(last, jnp.max(raw, axis=1, keepdims=True))
        row_ref[half] = peak
        wide = jnp.concatenate([peak] * groups, axis=1)
        phi = jnp.exp2((raw - wide) * slope).astype(jnp.bfloat16)
        part = dot_nt(phi, table_ref[slot])
        fade = jnp.exp2((last - peak) * slope + drop_ref[slot, 0:1, :])
        acc_ref[half] = acc_ref[half] * jnp.concatenate([fade, fade], axis=1) + part

    def finish(half):
        numer = acc_ref[half, :, 0:size]
        denom = acc_ref[half, :, size:2 * size]
        denom = denom + pltpu.roll(denom, size // 2, 1)
        return (numer / denom).astype(jnp.bfloat16)

    def step(t, carry):
        @pl.when(t < chunks)
        def _():
            pltpu.make_async_copy(w_ref.at[t], w_ref.at[t], w_recv.at[t]).wait()
            key_unit(0, t)

        @pl.when(t == ahead)
        def _():
            x_copies[0].wait_recv()
            x_copies[1].wait_recv()
            make_diag(1)

        @pl.when((t >= ahead) & (t < ahead + chunks))
        def _():
            key_unit(1, t - ahead)
            for copy in state_copies(t - ahead):
                copy.start()

        @pl.when(t == ahead + behind)
        def _():
            own_loads[2].wait()
            x_copies[2].wait_recv()

        @pl.when((t >= ahead + behind) & (t < ahead + behind + chunks))
        def _():
            slot = t - ahead - behind
            for copy in state_copies(slot):
                copy.wait_recv()
            combine(slot)
            query_unit(1, slot)

        @pl.when(t == ahead + behind + chunks - 1)
        def _():
            result_ref[...] = finish(1)
            out_copy.start()

        @pl.when(t >= ahead + behind + late)
        def _():
            query_unit(0, t - ahead - behind - late)

        return carry

    out_copy = pltpu.make_async_remote_copy(
        src_ref=result_ref, dst_ref=out_ref.at[side], send_sem=o_send, recv_sem=o_recv,
        device_id={"seq": x_mate}, device_id_type=MESH)
    own_loads[0].wait()
    own_loads[1].wait()
    make_diag(0)
    lax.fori_loop(0, chunks + ahead + behind + late, step, 0)
    out_ref[side] = finish(0)
    for copy in x_copies:
        copy.wait_send()
    for copy in w_copies:
        copy.wait_send()

    def drain(t, carry):
        for copy in state_copies(t):
            copy.wait_send()
        return carry

    lax.fori_loop(0, chunks, drain, 0)
    out_copy.wait()


def paired_shards(chunks, queries, key_vectors, values, projections):
    tokens, _, size = queries.shape
    width = projections.shape[1]
    scale = size ** -0.25
    start = lax.axis_index("feat") * 2
    pair = [lax.dynamic_slice_in_dim(a, start, 2, 1) for a in (queries, key_vectors, values)]
    own_q, own_k = (jnp.transpose(a, (1, 0, 2)) for a in pair[:2])
    own_v = jnp.transpose(pair[2], (1, 2, 0))
    bf16, f32 = jnp.bfloat16, jnp.float32
    dma = pltpu.SemaphoreType.DMA
    out = pl.pallas_call(
        functools.partial(head_kernel, chunks, AHEAD, BEHIND, LATE, scale),
        out_shape=jax.ShapeDtypeStruct((2, tokens, size), bf16),
        in_specs=[pl.BlockSpec(memory_space=pl.ANY)] * 4,
        out_specs=pl.BlockSpec(memory_space=pltpu.VMEM),
        scratch_shapes=[
            pltpu.VMEM((2, tokens, size), bf16),
            pltpu.VMEM((2, tokens, size), bf16),
            pltpu.VMEM((2, size, tokens), bf16),
            pltpu.VMEM((2, tokens, size), bf16),
            pltpu.VMEM((chunks, width, size), bf16),
            pltpu.VMEM((chunks, size + 16, width), f32),
            pltpu.VMEM((chunks, 8, width), f32),
            pltpu.VMEM((chunks, size, width), bf16),
            pltpu.VMEM((chunks, size, width), bf16),
            pltpu.VMEM((chunks, 2 * (width // size), size), f32),
            pltpu.VMEM((chunks, 2 * (width // size), size), f32),
            pltpu.VMEM((2, tokens, 2 * size), f32),
            pltpu.VMEM((2, tokens, size), f32),
            pltpu.VMEM((8, size), f32),
            pltpu.VMEM((chunks, 8, size), f32),
            pltpu.VMEM((chunks, 2 * size, width), bf16),
            pltpu.VMEM((tokens, size), bf16),
            dma((3,)), dma((3,)), dma((3,)), dma((chunks,)), dma((chunks,)),
            dma((2, chunks)), dma((2, chunks)), dma, dma,
        ],
        compiler_params=pltpu.CompilerParams(
            collective_id=0, has_side_effects=True, vmem_limit_bytes=60 * 1024 * 1024),
        name="favor_heads",
    )(own_q, own_k, own_v, projections)
    return jnp.transpose(out, (1, 0, 2))


def pairs_fit(mesh, args):
    queries, _, _, projections = args
    seq, feat = mesh.shape["seq"], mesh.shape["feat"]
    width = projections.shape[1] // feat
    tokens, size = queries.shape[0] // seq, queries.shape[2]
    return (seq == 4 and feat & (feat - 1) == 0 and queries.shape[1] == 2 * feat
            and size == 128 and width % size == 0 and tokens % 16 == 0)


def solution(mesh):
    placed = (
        P("seq", None, None),
        P("seq", None, None),
        P("seq", None, None),
        P(None, "feat", None),
    )

    def run(*args):
        body = functools.partial(paired_shards, mesh.shape["feat"]) if pairs_fit(mesh, args) else shards
        return jax.shard_map(
            body, mesh=mesh, in_specs=placed, out_specs=P("seq", "feat", None), check_vma=False
        )(*args)

    return run
```
